512 devices in a mesh: dp: 32 (over x, y, core), mp: 16 (over z).
Axes of the slice: x: 4, y: 4, z: 16, core: 2. Of those that a mesh axis runs over, the one named last changes fastest.
Arguments:
- patches: bfloat16 [512, 128, 1536], P(('dp', 'mp')), may hold values from -6 to 6
- keep_index: int32 [512, 128], P(('dp', 'mp')), may hold values from 0 to 127, each once within a row
- visible: int32 [512], P(('dp', 'mp')), may hold values from 16 to 80, as said below
- targets: bfloat16 [512, 12288], P(('dp', 'mp')), may hold values from -6 to 6
- w_up: bfloat16 [1536, 6144], P(None, 'mp'), may hold values from -0.15625 to 0.15625
- w_down: bfloat16 [6144, 1536], P('mp'), may hold values from -0.078125 to 0.078125
- dec_embed: bfloat16 [1536, 512], P('mp'), may hold values from -0.15625 to 0.15625
- dec_qkv: bfloat16 [512, 1536], P('mp'), may hold values from -1.45840774 to 1.45840774
- dec_out: bfloat16 [512, 512], P('mp'), may hold values from -0.25 to 0.25
- dec_pred: bfloat16 [512, 96], P('mp'), may hold values from -0.25 to 0.25
- mask_token: bfloat16 [512], replicated, may hold values from -4 to 4
- position: bfloat16 [128, 512], replicated, may hold values from -4.5 to 4.5
Outputs:
- recon: bfloat16 [512, 12288], P(('dp', 'mp'))
- patch_loss: float32 [512, 128], P(('dp', 'mp'))
The draws below stay inside these ranges and needn't reach their ends.
Inputs may be any that keep to these rules, and one draw needn't show every extreme that they name: For c < 256, visible[c] + visible[c + 256] = 96; some crop has exactly 80 visible patches.
All inputs are finite; a program needn't handle non-finite values.
Results may differ from the reference program's by a relative error of at most 0.04.
Values may be sent and summed in bfloat16 or wider, within the bound.
A program may use at most 64 MiB of HBM per device.

```python
import math
import jax
import jax.numpy as jnp
from jax import lax

D = 1536
FF = 6144
DD = 512
HSIZE = 64
P_SIZE = 128
PIX = 96
VMAX = 80
VMEAN = 48
CROPS = 512
N_MP = 16


def draw_visible(key, part):
    half = CROPS // 2
    first = jax.random.randint(key, (half,), 2 * VMEAN - VMAX, VMAX + 1, dtype=jnp.int32)
    first = first.at[0].set(VMAX)
    return jnp.concatenate([first, 2 * VMEAN - first]).astype(jnp.int32)


def draw_dec_qkv(key, part):
    limit = 32.0 / math.sqrt(DD)
    base = jnp.clip(jax.random.normal(key, (DD, 3 * DD), jnp.float32), -4.0, 4.0) * (1.0 / math.sqrt(DD))
    return jnp.clip(base, -limit, limit).astype(jnp.bfloat16)


def draw_position(key, part):
    base = jnp.clip(jax.random.normal(key, (P_SIZE, DD), jnp.float32), -4.0, 4.0)
    return base.astype(jnp.bfloat16)


def shard_levels(own_key, shape, split, smallest, largest):
    factor_of = 1.0
    for dim, blocks in split:
        draws = jax.random.uniform(jax.random.fold_in(jax.random.fold_in(own_key, 6), dim), (blocks,), jnp.float32, smallest / len(split), largest / len(split))
        factor_of = factor_of * jnp.repeat(jnp.exp(draws), shape[dim] // blocks).reshape((-1,) + (1,) * (len(shape) - 1 - dim))
    return factor_of


def bell_draw(stream_key, dims, scale, reach, pieces=(), kind=jnp.bfloat16):
    gain = shard_levels(stream_key, dims, pieces, -0.22, 0.18) if pieces else 1.0
    entries = jax.random.normal(stream_key, dims, jnp.float32) * scale * gain
    return jnp.minimum(jnp.maximum(entries, -reach), reach).astype(kind)


def setup_inputs(seed: int = 0) -> dict:
    key_of = jax.random.split(jax.random.key(seed), 13)
    patches = bell_draw(key_of[0], (CROPS, P_SIZE, D), 1.0, 6.0, ((0, 512),))
    keep_index = jax.vmap(lambda own: jax.random.permutation(own, P_SIZE))(jax.random.split(key_of[1], CROPS)).reshape((CROPS, P_SIZE)).astype(jnp.int32)
    visible = draw_visible(jax.random.fold_in(key_of[12], 71), 0)
    targets = bell_draw(key_of[3], (CROPS, P_SIZE * PIX), 1.0, 6.0, ((0, 512),))
    w_up = bell_draw(key_of[4], (D, FF), D ** -0.5, 0.15625, ((1, 16),))
    w_down = bell_draw(key_of[5], (FF, D), FF ** -0.5, 0.078125, ((0, 16),))
    dec_embed = bell_draw(key_of[6], (D, DD), D ** -0.5, 0.15625, ((0, 16),))
    dec_qkv = draw_dec_qkv(jax.random.fold_in(key_of[12], 71), 0)
    dec_out = bell_draw(key_of[8], (DD, DD), DD ** -0.5, 0.25, ((0, 16),))
    dec_pred = bell_draw(key_of[9], (DD, PIX), DD ** -0.5, 0.25, ((0, 16),))
    mask_token = bell_draw(key_of[10], (DD,), 1.0, 4.0)
    position = draw_position(jax.random.fold_in(key_of[12], 71), 0)
    return {"patches": patches, "keep_index": keep_index, "visible": visible, "targets": targets, "w_up": w_up, "w_down": w_down, "dec_embed": dec_embed, "dec_qkv": dec_qkv, "dec_out": dec_out, "dec_pred": dec_pred, "mask_token": mask_token, "position": position}


EPSILON = 1e-06

def layer_norm(values):
    center = values - lax.optimization_barrier(jnp.mean(values, axis=-1, keepdims=True))
    spread = lax.optimization_barrier(jnp.mean(center * center, axis=-1, keepdims=True))
    return center * lax.rsqrt(spread + EPSILON)

def multiply(left, right):
    return jnp.dot(left.astype(jnp.float32), right.astype(jnp.float32), precision=lax.Precision.HIGHEST)

def reference(patches, keep_index, visible, targets, w_up, w_down, dec_embed, dec_qkv, dec_out, dec_pred, mask_token, position):
    share = FF // N_MP
    heads = DD // HSIZE
    scale = 1.0 / math.sqrt(HSIZE)

    def one_crop(item):
        patch_rows, keep, count, target = item
        row_block = jnp.take(patch_rows, keep[:VMAX], axis=0)
        normed = layer_norm(row_block.astype(jnp.float32)).astype(jnp.bfloat16)
        hidden = jax.nn.gelu(multiply(normed, w_up), approximate=True).astype(jnp.bfloat16)
        summed = jnp.zeros((VMAX, D), jnp.float32)
        for shard in range(N_MP):
            partial_term = multiply(hidden[:, shard * share:(shard + 1) * share], w_down[shard * share:(shard + 1) * share]).astype(jnp.bfloat16)
            summed = summed + lax.optimization_barrier(partial_term).astype(jnp.float32)
        encoded = (row_block.astype(jnp.float32) + summed).astype(jnp.bfloat16)
        embedded = multiply(encoded, dec_embed).astype(jnp.bfloat16)
        slots = jnp.arange(P_SIZE, dtype=jnp.int32)
        inverse = jnp.zeros((P_SIZE,), jnp.int32).at[keep].set(slots)
        seen = inverse < count
        picked = jnp.take(embedded, jnp.minimum(inverse, VMAX - 1), axis=0).astype(jnp.float32)
        start = jnp.where(seen[:, None], picked, mask_token.astype(jnp.float32)[None, :]) + position.astype(jnp.float32)
        dec_normed = layer_norm(start).astype(jnp.bfloat16)
        projections = multiply(dec_normed, dec_qkv).astype(jnp.bfloat16)
        query = projections[:, :DD].reshape(P_SIZE, heads, HSIZE).astype(jnp.float32)
        keys = projections[:, DD:2 * DD].reshape(P_SIZE, heads, HSIZE).astype(jnp.float32)
        values = projections[:, 2 * DD:].reshape(P_SIZE, heads, HSIZE).astype(jnp.float32)
        scores = jnp.einsum('qhe,khe->hqk', query, keys, precision=lax.Precision.HIGHEST) * scale
        scores = scores - lax.optimization_barrier(jnp.max(scores, axis=-1, keepdims=True))
        weights = jnp.exp(scores)
        probs = (weights / lax.optimization_barrier(jnp.sum(weights, axis=-1, keepdims=True))).astype(jnp.bfloat16)
        mixed = jnp.einsum('hqk,khe->qhe', probs.astype(jnp.float32), values, precision=lax.Precision.HIGHEST)
        mixed = mixed.astype(jnp.bfloat16).reshape(P_SIZE, DD)
        after = start + multiply(mixed, dec_out)
        final = layer_norm(after).astype(jnp.bfloat16)
        prediction = multiply(final, dec_pred)
        error = prediction - target.reshape(P_SIZE, PIX).astype(jnp.float32)
        loss = jnp.where(seen, jnp.zeros((P_SIZE,), jnp.float32), lax.optimization_barrier(jnp.mean(error * error, axis=-1)))
        return (prediction.astype(jnp.bfloat16).reshape(P_SIZE * PIX), loss)
    recon, patch_loss = lax.map(one_crop, (patches, keep_index, visible, targets))
    return (recon, patch_loss)
```

```python
import functools
import math

import jax
import jax.numpy as jnp
from jax import lax
from jax.experimental import pallas as pl
from jax.experimental.pallas import tpu as pltpu
from jax.sharding import PartitionSpec as P

D = 1536
DD = 512
HSIZE = 64
PIX = 96
VMAX = 80
N_PATCH = 128
NZ = 16
SHARD = 384
LANES = 128
EPSILON = 1e-06
MESH = pl.DeviceIdType.MESH
F32 = jnp.float32
BF16 = jnp.bfloat16

EMBED_AT = 0
QKV_AT = 384
OUT_AT = 768
PRED_AT = 896
PACKED = 1024

UP_PIECE = 48
DOWN_PIECE = 144
CHUNKS = ((0, 48), (48, 32))


def z_slot(z):
    return (z % 4) * 4 + z // 4


def layer_norm(values):
    center = values - jnp.mean(values, axis=-1, keepdims=True)
    spread = jnp.mean(center * center, axis=-1, keepdims=True)
    return center * lax.rsqrt(spread + EPSILON)


def gelu(v):
    return 0.5 * v * (1.0 + jnp.tanh(math.sqrt(2.0 / math.pi) * (v + 0.044715 * v * v * v)))


def dot(a, b):
    return jnp.dot(a, b, preferred_element_type=F32)


def kernel(
    visible, keep_col, keep_row, patches, targets, mask_token, position,
    w_up, w_down, d_embed, d_qkv, d_out, d_pred,
    recon, loss,
    up, down, packed, up2, down2, dec, raw, slots, hidden, w2e, part, own, ret_out, ret_in, proj, mixed,
    load_sem, w_send, w_recv, d_send, d_recv, r_send, r_recv, b_send, b_recv,
):
    dp, z = lax.axis_index("dp"), lax.axis_index("mp")
    x, y, c = dp // 8, (dp // 2) % 4, dp % 2
    sign = 1 - 2 * c
    q_x = c * 16 + y * 4 + x
    q_y = c * 16 + x * 4 + y
    cls = z % 4
    q_z = jnp.where(cls < 2, q_x, q_y)

    def at_z(step):
        return (dp, (z + step + 2 * NZ) % NZ)

    def at_x(step):
        return (((x + step) % 4) * 8 + y * 2 + c, z)

    def at_y(step):
        return (x * 8 + ((y + step) % 4) * 2 + c, z)

    other_core = (x * 8 + y * 2 + (1 - c), z)
    ahead, behind = at_z(sign), at_z(-sign)

    barrier = pltpu.get_barrier_semaphore()
    greeted = [at_z(s) for s in (1, 2, 3, 4, 8, 12, 15)]
    greeted += [at_x(s) for s in (1, 2, 3)] + [at_y(s) for s in (1, 2, 3)] + [other_core]
    greeted_back = [at_z(s) for s in (13, 14)]
    for device in greeted + greeted_back:
        pl.semaphore_signal(barrier, inc=1, device_id=device, device_id_type=MESH)

    loads = []

    def load(src, dst):
        copy = pltpu.make_async_copy(src, dst, load_sem.at[len(loads)])
        copy.start()
        loads.append(copy)

    for j in range(4):
        load(d_embed.at[:, pl.ds(j * LANES, LANES)], packed.at[pl.ds(EMBED_AT + j * 96, 96)])
    for j in range(12):
        load(d_qkv.at[:, pl.ds(j * LANES, LANES)], packed.at[pl.ds(QKV_AT + j * 32, 32)])
    for j in range(4):
        load(d_out.at[:, pl.ds(j * LANES, LANES)], packed.at[pl.ds(OUT_AT + j * 32, 32)])
    load(d_pred, packed.at[pl.ds(PRED_AT, 32)])
    load(w_up, up)
    for j in range(12):
        load(w_down.at[:, pl.ds(j * LANES, LANES)], down.at[pl.ds(j * SHARD, SHARD)])
    packed[pl.ds(PRED_AT + 32, PACKED - PRED_AT - 32), :] = jnp.zeros((PACKED - PRED_AT - 32, LANES), BF16)

    chosen = keep_col[0:VMAX, :] == lax.broadcasted_iota(jnp.int32, (VMAX, N_PATCH), 1)
    picked = dot(chosen.astype(F32).astype(BF16), patches[...])
    raw[...] = picked.astype(BF16)
    slots[0] = layer_norm(picked).astype(BF16)

    for copy in loads:
        copy.wait()
    pl.semaphore_wait(barrier, len(greeted) + len(greeted_back))

    def send(src, dst, sems, index, device):
        copy = pltpu.make_async_remote_copy(
            src_ref=src, dst_ref=dst, send_sem=sems[0].at[index], recv_sem=sems[1].at[index],
            device_id=device, device_id_type=MESH,
        )
        copy.start()
        return copy

    sent = []

    def send_all(items, sems, first):
        copies = [send(src, dst, sems, first + i, device) for i, (src, dst, device) in enumerate(items)]
        sent.extend(copies)
        return copies

    def arrive(copies):
        for copy in copies:
            copy.wait_recv()

    wsem, dsem, rsem, bsem = (w_send, w_recv), (d_send, d_recv), (r_send, r_recv), (b_send, b_recv)

    def up_at(piece, count):
        return pl.ds(pl.multiple_of(piece * UP_PIECE, 16), count * UP_PIECE)

    def down_at(piece, count):
        return pl.ds(pl.multiple_of(piece * DOWN_PIECE, 16), count * DOWN_PIECE)

    w0 = send_all(
        [
            (up.at[up_at(q_x, 1)], up2.at[up_at(q_x, 1)], at_z(8)),
            (down.at[down_at(q_y, 1)], down2.at[down_at(q_y, 1)], at_z(8)),
        ],
        wsem, 0,
    )

    def rows_at(piece, count):
        return pl.ds(pl.multiple_of(piece * 32, 32), count * 32)

    mine = z_slot(z)
    dec[mine, rows_at(q_z, 1), :] = packed[rows_at(q_z, 1), :]
    d0 = send_all(
        [(packed.at[rows_at(q_z, 1)], dec.at[mine, rows_at(q_z, 1)], at_z(s)) for s in (4, 8, 12)], dsem, 0
    )

    def send_rows(k, side):
        first = 0 if side == 0 else 3
        src = 0 if k == 1 else first + k - 1
        dst = first + k
        return [
            (slots.at[src, pl.ds(at, n)], slots.at[dst, pl.ds(at, n)], ahead if side == 0 else behind)
            for at, n in CHUNKS
        ]

    def row_sem(k, side):
        return 2 * ((0 if side == 0 else 3) + k - 1)

    rows = {}

    def start_rows(k, side):
        rows[k, side] = send_all(send_rows(k, side), rsem, row_sem(k, side))

    def pass_rows(k):
        todo = [side for side in (0, 1) if (k, side) in rows]
        items = {side: send_rows(k + 1, side) for side in todo if k + 1 <= (3, 4)[side]}
        for side in items:
            rows[k + 1, side] = []
        for i in range(len(CHUNKS)):
            for side in todo:
                rows[k, side][i].wait_recv()
                if side in items:
                    rows[k + 1, side] += send_all([items[side][i]], rsem, row_sem(k + 1, side) + i)

    start_rows(1, 0)
    start_rows(1, 1)

    def hide(slot):
        hidden[slot, :, 0:SHARD] = gelu(dot(slots[slot], up[...])).astype(BF16)

    hide(0)

    arrive(d0)
    block = pl.ds(pl.multiple_of(cls * 4, 4), 4)
    d1 = send_all(
        [(dec.at[block, rows_at(q_z, 1)], dec.at[block, rows_at(q_z, 1)], at_z(s)) for s in (1, 2, 3)], dsem, 3
    )

    pass_rows(1)
    arrive(w0)
    w1 = send_all(
        [(up2.at[up_at(q_x, 1)], up2.at[up_at(q_x, 1)], at_x(s)) for s in (1, 2, 3)]
        + [(down2.at[down_at(q_y, 1)], down2.at[down_at(q_y, 1)], at_y(s)) for s in (1, 2, 3)],
        wsem, 2,
    )
    hide(1)
    hide(4)

    arrive(d1)
    low, high = pl.ds(0, 8), pl.ds(8, 8)
    d2 = send_all(
        [(dec.at[low, rows_at(q_x, 1)], dec.at[low, rows_at(q_x, 1)], at_x(s)) for s in (1, 2, 3)]
        + [(dec.at[high, rows_at(q_y, 1)], dec.at[high, rows_at(q_y, 1)], at_y(s)) for s in (1, 2, 3)],
        dsem, 6,
    )

    arrive(w1)
    q_xs, q_ys = c * 16 + y * 4, c * 16 + x * 4
    w2 = send_all(
        [(up2.at[up_at(q_xs, 4)], up2.at[up_at(q_xs, 4)], at_y(s)) for s in (1, 2, 3)]
        + [(down2.at[down_at(q_ys, 4)], down2.at[down_at(q_ys, 4)], at_x(s)) for s in (1, 2, 3)],
        wsem, 8,
    )

    pass_rows(2)
    hide(2)
    hide(5)

    arrive(d2)
    d3 = send_all(
        [(dec.at[low, rows_at(q_xs, 4)], dec.at[low, rows_at(q_xs, 4)], at_y(s)) for s in (1, 2, 3)]
        + [(dec.at[high, rows_at(q_ys, 4)], dec.at[high, rows_at(q_ys, 4)], at_x(s)) for s in (1, 2, 3)],
        dsem, 12,
    )

    arrive(w2)
    w3 = send_all(
        [
            (up2.at[up_at(c * 16, 16)], up2.at[up_at(c * 16, 16)], other_core),
            (down2.at[down_at(c * 16, 16)], down2.at[down_at(c * 16, 16)], other_core),
        ],
        wsem, 14,
    )

    pass_rows(3)
    hide(3)
    hide(6)

    arrive(d3)
    d4 = send_all([(dec.at[:, rows_at(c * 16, 16)], dec.at[:, rows_at(c * 16, 16)], other_core)], dsem, 18)

    def weight(at, rows_per, blocks):
        return jnp.concatenate(
            [
                jnp.concatenate(
                    [dec[z_slot(s), at + b * rows_per : at + (b + 1) * rows_per, :] for s in range(NZ)], axis=0
                )
                for b in blocks
            ],
            axis=1,
        )

    pass_rows(4)
    hide(7)
    arrive(w3)

    def hide_far(slot, carry):
        hidden[slot, :, SHARD : 2 * SHARD] = gelu(dot(slots[slot], up2[...])).astype(BF16)
        return carry

    lax.fori_loop(0, 8, hide_far, 0)

    arrive(d4)
    downs = [
        jnp.concatenate([ref[j * SHARD : (j + 1) * SHARD, :] for j in range(12)], axis=1) for ref in (down, down2)
    ]
    for half in (0, 1):
        embed = weight(EMBED_AT, 96, (2 * half, 2 * half + 1))
        cols = slice(256 * half, 256 * half + 256)
        for s in (0, 1):
            w2e[s * SHARD : (s + 1) * SHARD, cols] = dot(downs[s], embed).astype(BF16)
        own[:, cols] = dot(raw[...], embed)

    def partial(slot):
        return dot(hidden[slot], w2e[...])

    ret_out[3] = partial(7).astype(BF16)
    back = {(1, 0): send_all([(ret_out.at[3], ret_in.at[3], ahead)], bsem, 3)}
    ret_out[0] = partial(3).astype(BF16)
    back[0, 0] = send_all([(ret_out.at[0], ret_in.at[0], behind)], bsem, 0)
    own[...] += partial(0)

    def add_part(slot, carry):
        part[slot] = partial(slot)
        return carry

    lax.fori_loop(1, 7, add_part, 0)
    for step in (0, 1, 2):
        arrive(back[1, step])
        ret_out[4 + step] = (ret_in[3 + step].astype(F32) + part[6 - step]).astype(BF16)
        back[1, step + 1] = send_all([(ret_out.at[4 + step], ret_in.at[4 + step], ahead)], bsem, 4 + step)
        if step < 2:
            arrive(back[0, step])
            ret_out[1 + step] = (ret_in[step].astype(F32) + part[2 - step]).astype(BF16)
            back[0, step + 1] = send_all([(ret_out.at[1 + step], ret_in.at[1 + step], behind)], bsem, 1 + step)
    arrive(back[0, 2])
    arrive(back[1, 3])
    embedded = (own[...] + ret_in[2].astype(F32) + ret_in[6].astype(F32)).astype(BF16)

    count = visible[0]
    spread = (keep_row[...] == lax.broadcasted_iota(jnp.int32, (N_PATCH, N_PATCH), 0)) & (
        lax.broadcasted_iota(jnp.int32, (N_PATCH, N_PATCH), 1) < count
    )
    spread = jnp.where(spread, 1.0, 0.0)
    seen = jnp.sum(spread, axis=1, keepdims=True) > 0.5
    placed = dot(spread[:, 0:VMAX].astype(BF16), embedded)
    start = jnp.where(seen, placed, mask_token[...].astype(F32)) + position[...].astype(F32)
    normed = layer_norm(start).astype(BF16)
    for b in range(6):
        both = dot(normed, weight(QKV_AT, 32, (2 * b, 2 * b + 1))).astype(BF16)
        proj[2 * b] = both[:, 0:LANES]
        proj[2 * b + 1] = both[:, LANES : 2 * LANES]
    left = lax.broadcasted_iota(jnp.int32, (N_PATCH, LANES), 1) < HSIZE
    for b in range(4):
        query, keys, values = proj[b], proj[4 + b], proj[8 + b]
        outs = []
        for side in (left, jnp.logical_not(left)):
            one = jnp.where(side, query.astype(F32), 0.0).astype(BF16)
            scores = lax.dot_general(one, keys, (((1,), (1,)), ((), ())), preferred_element_type=F32)
            scores = scores * (1.0 / math.sqrt(HSIZE))
            weights = jnp.exp(scores - jnp.max(scores, axis=-1, keepdims=True))
            probs = (weights / jnp.sum(weights, axis=-1, keepdims=True)).astype(BF16)
            outs.append(dot(probs, values))
        mixed[:, b * LANES : (b + 1) * LANES] = jnp.where(left, outs[0], outs[1]).astype(BF16)
    after = start + jnp.concatenate(
        [dot(mixed[...], weight(OUT_AT, 32, (2 * b, 2 * b + 1))) for b in range(2)], axis=1
    )
    final = layer_norm(after).astype(BF16)
    prediction = dot(final, weight(PRED_AT, 32, (0,)))
    recon[...] = prediction.astype(BF16)
    error = prediction - targets[...].astype(F32)
    error = jnp.sum(error * error, axis=-1, keepdims=True) * (1.0 / PIX)
    loss[...] = jnp.where(seen, 0.0, error)

    for copy in sent:
        copy.wait_send()


def body(
    patches, keep_index, visible, targets, w_up, w_down, dec_embed, dec_qkv, dec_out, dec_pred, mask_token, position
):
    any_spec = pl.BlockSpec(memory_space=pl.ANY)
    vmem = pl.BlockSpec(memory_space=pltpu.VMEM)
    dma = pltpu.SemaphoreType.DMA
    recon, loss = pl.pallas_call(
        kernel,
        out_shape=(
            jax.ShapeDtypeStruct((N_PATCH, LANES), BF16),
            jax.ShapeDtypeStruct((N_PATCH, 1), F32),
        ),
        in_specs=[pl.BlockSpec(memory_space=pltpu.SMEM)] + [vmem] * 6 + [any_spec] * 6,
        out_specs=(vmem, vmem),
        scratch_shapes=[
            pltpu.VMEM((D, SHARD), BF16),
            pltpu.VMEM((12 * SHARD, LANES), BF16),
            pltpu.VMEM((PACKED, LANES), BF16),
            pltpu.VMEM((D, SHARD), BF16),
            pltpu.VMEM((12 * SHARD, LANES), BF16),
            pltpu.VMEM((NZ, PACKED, LANES), BF16),
            pltpu.VMEM((VMAX, D), BF16),
            pltpu.VMEM((8, VMAX, D), BF16),
            pltpu.VMEM((8, VMAX, 2 * SHARD), BF16),
            pltpu.VMEM((2 * SHARD, DD), BF16),
            pltpu.VMEM((8, VMAX, DD), F32),
            pltpu.VMEM((VMAX, DD), F32),
            pltpu.VMEM((7, VMAX, DD), BF16),
            pltpu.VMEM((7, VMAX, DD), BF16),
            pltpu.VMEM((12, N_PATCH, LANES), BF16),
            pltpu.VMEM((N_PATCH, DD), BF16),
            dma((34,)),
            dma((16,)),
            dma((16,)),
            dma((19,)),
            dma((19,)),
            dma((14,)),
            dma((14,)),
            dma((7,)),
            dma((7,)),
        ],
        compiler_params=pltpu.CompilerParams(
            collective_id=0, has_side_effects=True, vmem_limit_bytes=48 * 1024 * 1024
        ),
    )(
        visible,
        keep_index.reshape(N_PATCH, 1),
        keep_index,
        patches.reshape(N_PATCH, D),
        jnp.pad(targets.reshape(N_PATCH, PIX), ((0, 0), (0, LANES - PIX))),
        mask_token.reshape(1, DD),
        position,
        w_up,
        w_down,
        dec_embed,
        dec_qkv,
        dec_out,
        jnp.pad(dec_pred, ((0, 0), (0, LANES - PIX))),
    )
    return (recon[:, :PIX].reshape(1, N_PATCH * PIX), loss.reshape(1, N_PATCH))


def solution(mesh):
    return jax.shard_map(
        body,
        mesh=mesh,
        in_specs=(
            P(("dp", "mp"), None, None),
            P(("dp", "mp"), None),
            P(("dp", "mp")),
            P(("dp", "mp"), None),
            P(None, "mp"),
            P("mp", None),
            P("mp", None),
            P("mp", None),
            P("mp", None),
            P("mp", None),
            P(),
            P(),
        ),
        out_specs=(P(("dp", "mp"), None), P(("dp", "mp"), None)),
        check_vma=False,
    )
```

```python
import functools
import math

import jax
import jax.numpy as jnp
from jax import lax
from jax.experimental import pallas as pl
from jax.experimental.pallas import tpu as pltpu
from jax.sharding import PartitionSpec as P

D = 1536
DD = 512
HSIZE = 64
PIX = 96
VMAX = 80
N_PATCH = 128
NZ = 16
SHARD = 384
LANES = 128
EPSILON = 1e-06
MESH = pl.DeviceIdType.MESH
F32 = jnp.float32
BF16 = jnp.bfloat16

EMBED_AT = 0
QKV_AT = 384
OUT_AT = 768
PRED_AT = 896
PACKED = 1024

UP_PIECE = 48
CHUNKS = ((0, 48), (48, 32))


def z_slot(z):
    return (z % 4) * 4 + z // 4


def layer_norm(values):
    center = values - jnp.mean(values, axis=-1, keepdims=True)
    spread = jnp.mean(center * center, axis=-1, keepdims=True)
    return center * lax.rsqrt(spread + EPSILON)


def gelu(v):
    return 0.5 * v * (1.0 + jnp.tanh(math.sqrt(2.0 / math.pi) * (v + 0.044715 * v * v * v)))


def dot(a, b):
    return jnp.dot(a, b, preferred_element_type=F32)


def kernel(
    visible_hbm, keep_hbm, patches_hbm, targets_hbm, mask_hbm, position_hbm,
    w_up, w_down, d_embed, d_qkv, d_out, d_pred,
    recon, loss,
    visible, keep, patches, targets, mask_token, position, pred,
    up, down, packed, up2, down2, dec, raw, slots, hidden, w2e, part, own, ret_out, ret_in, proj, mixed,
    load_sem, w_send, w_recv, d_send, d_recv, r_send, r_recv, b_send, b_recv,
):
    dp, z = lax.axis_index("dp"), lax.axis_index("mp")
    x, y, c = dp // 8, (dp // 2) % 4, dp % 2
    sign = 1 - 2 * c
    q_x = c * 16 + y * 4 + x
    q_y = c * 16 + x * 4 + y
    cls = z % 4
    q_z = jnp.where(cls < 2, q_x, q_y)

    def at_z(step):
        return (dp, (z + step + 2 * NZ) % NZ)

    def at_x(step):
        return (((x + step) % 4) * 8 + y * 2 + c, z)

    def at_y(step):
        return (x * 8 + ((y + step) % 4) * 2 + c, z)

    other_core = (x * 8 + y * 2 + (1 - c), z)
    ahead, behind = at_z(sign), at_z(-sign)

    barrier = pltpu.get_barrier_semaphore()
    greeted = [at_z(s) for s in (8, 4, 12, 3, 13, 2, 14, 1, 15)]
    greeted += [at_x(s) for s in (2, 1, 3)] + [at_y(s) for s in (2, 1, 3)] + [other_core]
    for device in greeted:
        pl.semaphore_signal(barrier, inc=1, device_id=device, device_id_type=MESH)

    n_loads = [0]

    def load(src, dst):
        copy = pltpu.make_async_copy(src, dst, load_sem.at[n_loads[0]])
        n_loads[0] += 1
        copy.start()
        return copy

    first_loads = [load(keep_hbm, keep), load(patches_hbm.at[0], patches)]
    pack_loads = [
        load(d_embed.at[:, pl.ds(j * LANES, LANES)], packed.at[pl.ds(EMBED_AT + j * 96, 96)]) for j in range(4)
    ]
    pack_loads += [
        load(d_qkv.at[:, pl.ds(j * LANES, LANES)], packed.at[pl.ds(QKV_AT + j * 32, 32)]) for j in range(12)
    ]
    pack_loads += [
        load(d_out.at[:, pl.ds(j * LANES, LANES)], packed.at[pl.ds(OUT_AT + j * 32, 32)]) for j in range(4)
    ]
    pack_loads += [load(d_pred, pred)]
    up_load, down_load = load(w_up, up), load(w_down, down)
    late_loads = [
        load(visible_hbm, visible), load(targets_hbm, targets), load(mask_hbm, mask_token), load(position_hbm, position)
    ]

    for copy in first_loads:
        copy.wait()
    patch_of = lax.broadcasted_iota(jnp.int32, (N_PATCH, N_PATCH), 0)
    chosen = jnp.where(keep[...] == patch_of, 1.0, 0.0)
    picked = dot(jnp.transpose(chosen)[0:VMAX, :].astype(BF16), patches[...])
    raw[...] = picked.astype(BF16)
    slots[0] = layer_norm(picked).astype(BF16)

    for copy in pack_loads:
        copy.wait()
    packed[pl.ds(PRED_AT, 32), :] = jnp.concatenate([pred[...], jnp.zeros((32, LANES - PIX), BF16)], axis=1)
    packed[pl.ds(PRED_AT + 32, PACKED - PRED_AT - 32), :] = jnp.zeros((PACKED - PRED_AT - 32, LANES), BF16)
    pl.semaphore_wait(barrier, len(greeted))

    def send(src, dst, sems, index, device):
        copy = pltpu.make_async_remote_copy(
            src_ref=src, dst_ref=dst, send_sem=sems[0].at[index], recv_sem=sems[1].at[index],
            device_id=device, device_id_type=MESH,
        )
        copy.start()
        return copy

    sent = []

    def send_all(items, sems, first):
        copies = [send(src, dst, sems, first + i, device) for i, (src, dst, device) in enumerate(items)]
        sent.extend(copies)
        return copies

    def arrive(copies):
        for copy in copies:
            copy.wait_recv()

    wsem, dsem, rsem, bsem = (w_send, w_recv), (d_send, d_recv), (r_send, r_recv), (b_send, b_recv)

    def up_at(piece, count):
        return pl.ds(pl.multiple_of(piece * UP_PIECE, 16), count * UP_PIECE)

    def group(i, count):
        return pl.ds(pl.multiple_of(i * 48, 16), count * 48)

    cell = (group(c * 4 + x, 1), pl.ds(pl.multiple_of(y * SHARD, LANES), SHARD))
    w0 = send_all(
        [(w_up.at[up_at(q_x, 1)], up2.at[up_at(q_x, 1)], at_z(8)), (w_down.at[cell], down2.at[cell], at_z(8))],
        wsem, 0,
    )

    def rows_at(piece, count):
        return pl.ds(pl.multiple_of(piece * 32, 32), count * 32)

    mine = z_slot(z)
    dec[mine, rows_at(q_z, 1), :] = packed[rows_at(q_z, 1), :]
    d0 = send_all(
        [(packed.at[rows_at(q_z, 1)], dec.at[mine, rows_at(q_z, 1)], at_z(s)) for s in (4, 8, 12)], dsem, 0
    )

    def slot_of(k, side):
        return 0 if k == 0 else (7 if k == 4 else 2 * k - 1 + side)

    def send_rows(k, side):
        src, dst = slot_of(k - 1, side), slot_of(k, side)
        return [
            (slots.at[src, pl.ds(at, n)], slots.at[dst, pl.ds(at, n)], ahead if side == 0 else behind)
            for at, n in CHUNKS
        ]

    def row_sem(k, side):
        return 2 * (slot_of(k, side) - 1)

    rows = {}

    def start_rows(k, side):
        rows[k, side] = send_all(send_rows(k, side), rsem, row_sem(k, side))

    def pass_rows(k):
        todo = [side for side in (0, 1) if (k, side) in rows]
        items = {side: send_rows(k + 1, side) for side in todo if k + 1 <= (3, 4)[side]}
        for side in items:
            rows[k + 1, side] = []
        for i in range(len(CHUNKS)):
            for side in todo:
                rows[k, side][i].wait_recv()
                if side in items:
                    rows[k + 1, side] += send_all([items[side][i]], rsem, row_sem(k + 1, side) + i)

    start_rows(1, 0)
    start_rows(1, 1)
    up_load.wait()

    def hide(slot, count=1):
        block = slots[slot : slot + count].reshape(count * VMAX, D)
        part = gelu(dot(block, up[...])).astype(BF16)
        hidden[slot : slot + count, :, 0:SHARD] = part.reshape(count, VMAX, SHARD)

    hide(0)

    arrive(d0)
    block = pl.ds(pl.multiple_of(cls * 4, 4), 4)
    d1 = send_all(
        [(dec.at[block, rows_at(q_z, 1)], dec.at[block, rows_at(q_z, 1)], at_z(s)) for s in (1, 2, 3)], dsem, 3
    )

    pass_rows(1)
    arrive(w0)
    w1 = send_all(
        [(up2.at[up_at(q_x, 1)], up2.at[up_at(q_x, 1)], at_x(s)) for s in (1, 2, 3)]
        + [(down2.at[cell], down2.at[cell], at_y(s)) for s in (1, 2, 3)],
        wsem, 2,
    )
    hide(1, 2)

    arrive(d1)
    low, high = pl.ds(0, 8), pl.ds(8, 8)
    d2 = send_all(
        [(dec.at[low, rows_at(q_x, 1)], dec.at[low, rows_at(q_x, 1)], at_x(s)) for s in (1, 2, 3)]
        + [(dec.at[high, rows_at(q_y, 1)], dec.at[high, rows_at(q_y, 1)], at_y(s)) for s in (1, 2, 3)],
        dsem, 6,
    )

    arrive(w1)
    q_xs, q_ys = c * 16 + y * 4, c * 16 + x * 4
    w2 = send_all(
        [(up2.at[up_at(q_xs, 4)], up2.at[up_at(q_xs, 4)], at_y(s)) for s in (1, 2, 3)]
        + [(down2.at[group(c * 4 + x, 1)], down2.at[group(c * 4 + x, 1)], at_x(s)) for s in (1, 2, 3)],
        wsem, 8,
    )

    pass_rows(2)
    hide(3, 2)

    arrive(d2)
    d3 = send_all(
        [(dec.at[low, rows_at(q_xs, 4)], dec.at[low, rows_at(q_xs, 4)], at_y(s)) for s in (1, 2, 3)]
        + [(dec.at[high, rows_at(q_ys, 4)], dec.at[high, rows_at(q_ys, 4)], at_x(s)) for s in (1, 2, 3)],
        dsem, 12,
    )

    arrive(w2)
    w3 = send_all(
        [
            (up2.at[up_at(c * 16, 16)], up2.at[up_at(c * 16, 16)], other_core),
            (down2.at[group(c * 4, 4)], down2.at[group(c * 4, 4)], other_core),
        ],
        wsem, 14,
    )

    pass_rows(3)
    hide(5, 2)

    arrive(d3)
    d4 = send_all([(dec.at[:, rows_at(c * 16, 16)], dec.at[:, rows_at(c * 16, 16)], other_core)], dsem, 18)

    def weight(at, rows_per, blocks):
        return jnp.concatenate(
            [
                jnp.concatenate(
                    [dec[z_slot(s), at + b * rows_per : at + (b + 1) * rows_per, :] for s in range(NZ)], axis=0
                )
                for b in blocks
            ],
            axis=1,
        )

    down_load.wait()
    for copy in late_loads:
        copy.wait()
    pass_rows(4)
    hide(7)
    arrive(w3)

    def hide_far(i, carry):
        block = slots[pl.ds(2 * i, 2)].reshape(2 * VMAX, D)
        part = gelu(dot(block, up2[...])).astype(BF16)
        hidden[pl.ds(2 * i, 2), :, SHARD : 2 * SHARD] = part.reshape(2, VMAX, SHARD)
        return carry

    lax.fori_loop(0, 4, hide_far, 0)

    arrive(d4)
    for half in (0, 1):
        embed = weight(EMBED_AT, 96, (2 * half, 2 * half + 1))
        cols = slice(256 * half, 256 * half + 256)
        for s, shard in enumerate((down, down2)):
            w2e[s * SHARD : (s + 1) * SHARD, cols] = dot(shard[...], embed).astype(BF16)
        own[:, cols] = dot(raw[...], embed)

    def partial(slot):
        return dot(hidden[slot], w2e[...])

    ret_out[3] = partial(slot_of(4, 1)).astype(BF16)
    back = {(1, 0): send_all([(ret_out.at[3], ret_in.at[3], ahead)], bsem, 3)}
    ret_out[0] = partial(slot_of(3, 0)).astype(BF16)
    back[0, 0] = send_all([(ret_out.at[0], ret_in.at[0], behind)], bsem, 0)
    own[...] += partial(0)

    def add_part(slot, carry):
        part[slot] = partial(slot)
        return carry

    lax.fori_loop(1, 7, add_part, 0)
    for step in (0, 1, 2):
        arrive(back[1, step])
        ret_out[4 + step] = (ret_in[3 + step].astype(F32) + part[slot_of(3 - step, 1)]).astype(BF16)
        back[1, step + 1] = send_all([(ret_out.at[4 + step], ret_in.at[4 + step], ahead)], bsem, 4 + step)
        if step < 2:
            arrive(back[0, step])
            ret_out[1 + step] = (ret_in[step].astype(F32) + part[slot_of(2 - step, 0)]).astype(BF16)
            back[0, step + 1] = send_all([(ret_out.at[1 + step], ret_in.at[1 + step], behind)], bsem, 1 + step)

    count = visible[0]
    row = lax.broadcasted_iota(jnp.int32, (N_PATCH, N_PATCH), 0)
    lane = lax.broadcasted_iota(jnp.int32, (N_PATCH, N_PATCH), 1)
    patch = 4 * (row % 32) + row // 32
    spread = jnp.where((keep[...] == patch) & (lane < count), 1.0, 0.0)
    seen = jnp.sum(spread, axis=1, keepdims=True) > 0.5
    spread = spread[:, 0:VMAX].astype(BF16)
    order = jnp.where(lane == patch, 1.0, 0.0)
    places = dot(order.astype(BF16), position[...])
    masked = mask_token[...].astype(F32).reshape(1, DD)

    arrive(back[0, 2])
    arrive(back[1, 3])
    embedded = (own[...] + ret_in[2].astype(F32) + ret_in[6].astype(F32)).astype(BF16)
    start = jnp.where(seen, dot(spread, embedded), masked) + places
    normed = layer_norm(start).astype(BF16)
    for b in range(6):
        both = dot(normed, weight(QKV_AT, 32, (2 * b, 2 * b + 1))).astype(BF16)
        proj[2 * b] = both[:, 0:LANES]
        proj[2 * b + 1] = both[:, LANES : 2 * LANES]
    left = lane < HSIZE
    for b in range(4):
        query, keys, values = proj[b], proj[4 + b], proj[8 + b]
        outs = []
        for side in (left, jnp.logical_not(left)):
            one = jnp.where(side, query.astype(F32), 0.0).astype(BF16)
            scores = lax.dot_general(one, keys, (((1,), (1,)), ((), ())), preferred_element_type=F32)
            scores = scores * (1.0 / math.sqrt(HSIZE))
            weights = jnp.exp(scores - jnp.max(scores, axis=-1, keepdims=True))
            probs = (weights / jnp.sum(weights, axis=-1, keepdims=True)).astype(BF16)
            outs.append(dot(probs, values))
        mixed[:, b * LANES : (b + 1) * LANES] = jnp.where(left, outs[0], outs[1]).astype(BF16)
    after = start + jnp.concatenate(
        [dot(mixed[...], weight(OUT_AT, 32, (2 * b, 2 * b + 1))) for b in range(2)], axis=1
    )
    final = layer_norm(after).astype(BF16)
    prediction = dot(final, weight(PRED_AT, 32, (0,)))

    turned = [pltpu.roll(prediction[32 * r : 32 * r + 32, :], (PIX * r) % LANES, 1) if r else prediction[0:32, :] for r in range(4)]
    lane = lane[0:32, :]
    edges = (96, 64, 32)
    pixels = [jnp.where(lane < edges[b], turned[b], turned[b + 1]) for b in range(3)]
    sums = [0.0] * 4
    for b in range(3):
        wide = pixels[b].astype(BF16)
        wanted = []
        for g in range(32):
            at = slice(384 * g + LANES * b, 384 * g + LANES * b + LANES)
            recon[:, at] = wide[g : g + 1, :]
            wanted.append(targets[:, at])
        error = pixels[b] - jnp.concatenate(wanted, axis=0).astype(F32)
        error = error * error
        sums[b] += jnp.sum(jnp.where(lane < edges[b], error, 0.0), axis=-1, keepdims=True)
        sums[b + 1] += jnp.sum(jnp.where(lane < edges[b], 0.0, error), axis=-1, keepdims=True)
    per_row = jnp.where(seen, 0.0, jnp.concatenate(sums, axis=0) * (1.0 / PIX))
    loss[...] = jnp.sum(order * per_row, axis=0, keepdims=True)

    for copy in sent:
        copy.wait_send()


def body(
    patches, keep_index, visible, targets, w_up, w_down, dec_embed, dec_qkv, dec_out, dec_pred, mask_token, position
):
    hbm = pl.BlockSpec(memory_space=pltpu.HBM)
    vmem = pl.BlockSpec(memory_space=pltpu.VMEM)
    dma = pltpu.SemaphoreType.DMA
    return pl.pallas_call(
        kernel,
        out_shape=(
            jax.ShapeDtypeStruct((1, N_PATCH * PIX), BF16),
            jax.ShapeDtypeStruct((1, N_PATCH), F32),
        ),
        in_specs=[hbm] * 12,
        out_specs=(vmem, vmem),
        scratch_shapes=[
            pltpu.SMEM((1,), jnp.int32),
            pltpu.VMEM((1, N_PATCH), jnp.int32),
            pltpu.VMEM((N_PATCH, D), BF16),
            pltpu.VMEM((1, N_PATCH * PIX), BF16),
            pltpu.VMEM((DD,), BF16),
            pltpu.VMEM((N_PATCH, DD), BF16),
            pltpu.VMEM((32, PIX), BF16),
            pltpu.VMEM((D, SHARD), BF16),
            pltpu.VMEM((SHARD, D), BF16),
            pltpu.VMEM((PACKED, LANES), BF16),
            pltpu.VMEM((D, SHARD), BF16),
            pltpu.VMEM((SHARD, D), BF16),
            pltpu.VMEM((NZ, PACKED, LANES), BF16),
            pltpu.VMEM((VMAX, D), BF16),
            pltpu.VMEM((8, VMAX, D), BF16),
            pltpu.VMEM((8, VMAX, 2 * SHARD), BF16),
            pltpu.VMEM((2 * SHARD, DD), BF16),
            pltpu.VMEM((8, VMAX, DD), F32),
            pltpu.VMEM((VMAX, DD), F32),
            pltpu.VMEM((7, VMAX, DD), BF16),
            pltpu.VMEM((7, VMAX, DD), BF16),
            pltpu.VMEM((12, N_PATCH, LANES), BF16),
            pltpu.VMEM((N_PATCH, DD), BF16),
            dma((29,)),
            dma((16,)),
            dma((16,)),
            dma((19,)),
            dma((19,)),
            dma((14,)),
            dma((14,)),
            dma((7,)),
            dma((7,)),
        ],
        compiler_params=pltpu.CompilerParams(
            collective_id=0, has_side_effects=True, vmem_limit_bytes=56 * 1024 * 1024
        ),
    )(
        visible, keep_index, patches, targets, mask_token, position,
        w_up, w_down, dec_embed, dec_qkv, dec_out, dec_pred,
    )


def solution(mesh):
    return jax.shard_map(
        body,
        mesh=mesh,
        in_specs=(
            P(("dp", "mp"), None, None),
            P(("dp", "mp"), None),
            P(("dp", "mp")),
            P(("dp", "mp"), None),
            P(None, "mp"),
            P("mp", None),
            P("mp", None),
            P("mp", None),
            P("mp", None),
            P("mp", None),
            P(),
            P(),
        ),
        out_specs=(P(("dp", "mp"), None), P(("dp", "mp"), None)),
        check_vma=False,
    )
```

```python
import functools
import math

import jax
import jax.numpy as jnp
from jax import lax
from jax.experimental import pallas as pl
from jax.experimental.pallas import tpu as pltpu
from jax.sharding import PartitionSpec as P

D = 1536
DD = 512
HSIZE = 64
PIX = 96
VMAX = 80
N_PATCH = 128
NZ = 16
SHARD = 384
LANES = 128
EPSILON = 1e-06
MESH = pl.DeviceIdType.MESH
F32 = jnp.float32
BF16 = jnp.bfloat16

EMBED_AT = 0
PRED_AT = 384
QKV_AT = 512
OUT_AT = 896
PACKED = 1024
HALF = 512

UP_PIECE = 48
CHUNKS = ((0, 48), (48, 32))


def z_slot(z):
    return (z % 4) * 4 + z // 4


def layer_norm(values):
    center = values - jnp.mean(values, axis=-1, keepdims=True)
    spread = jnp.mean(center * center, axis=-1, keepdims=True)
    return center * lax.rsqrt(spread + EPSILON)


def gelu(v):
    return 0.5 * v * (1.0 + jnp.tanh(math.sqrt(2.0 / math.pi) * (v + 0.044715 * v * v * v)))


def dot(a, b):
    return jnp.dot(a, b, preferred_element_type=F32)


def kernel(
    visible_hbm, keep_hbm, patches_hbm, targets_hbm, mask_hbm, position_hbm,
    w_up, w_down, d_embed, d_qkv, d_out, d_pred,
    recon, loss,
    visible, keep, patches, targets, mask_token, position, pred,
    up, down, packed, up2, down2, dec, raw, slots, hidden, w2e, part, own, ret_out, ret_in, proj, mixed,
    load_sem, w_send, w_recv, d_send, d_recv, r_send, r_recv, b_send, b_recv,
):
    dp, z = lax.axis_index("dp"), lax.axis_index("mp")
    x, y, c = dp // 8, (dp // 2) % 4, dp % 2
    sign = 1 - 2 * c
    q_x = c * 16 + y * 4 + x
    q_y = c * 16 + x * 4 + y
    cls = z % 4
    q_z = jnp.where(cls < 2, q_x, q_y)
    q_xs, q_ys = c * 16 + y * 4, c * 16 + x * 4

    def at_z(step):
        return (dp, (z + step + 2 * NZ) % NZ)

    def at_x(step):
        return (((x + step) % 4) * 8 + y * 2 + c, z)

    def at_y(step):
        return (x * 8 + ((y + step) % 4) * 2 + c, z)

    other_core = (x * 8 + y * 2 + (1 - c), z)
    ahead, behind = at_z(sign), at_z(-sign)

    barrier = pltpu.get_barrier_semaphore()
    greeted = [at_z(s) for s in (8, 4, 12, 3, 13, 2, 14, 1, 15)]
    greeted += [at_x(s) for s in (2, 1, 3)] + [at_y(s) for s in (2, 1, 3)] + [other_core]
    for device in greeted:
        pl.semaphore_signal(barrier, inc=1, device_id=device, device_id_type=MESH)

    n_loads = [0]

    def load(src, dst):
        copy = pltpu.make_async_copy(src, dst, load_sem.at[n_loads[0]])
        n_loads[0] += 1
        copy.start()
        return copy

    first_loads = [load(keep_hbm, keep), load(patches_hbm.at[0], patches)]
    pack_loads = [
        load(d_embed.at[:, pl.ds(j * LANES, LANES)], packed.at[pl.ds(EMBED_AT + j * 96, 96)]) for j in range(4)
    ]
    pack_loads += [
        load(d_qkv.at[:, pl.ds(j * LANES, LANES)], packed.at[pl.ds(QKV_AT + j * 32, 32)]) for j in range(12)
    ]
    pack_loads += [
        load(d_out.at[:, pl.ds(j * LANES, LANES)], packed.at[pl.ds(OUT_AT + j * 32, 32)]) for j in range(4)
    ]
    pack_loads += [load(d_pred, pred)]
    up_load, down_load = load(w_up, up), load(w_down, down)
    late_loads = [
        load(visible_hbm, visible), load(targets_hbm, targets), load(mask_hbm, mask_token), load(position_hbm, position)
    ]

    for copy in first_loads:
        copy.wait()
    patch_of = lax.broadcasted_iota(jnp.int32, (N_PATCH, N_PATCH), 0)
    chosen = jnp.where(keep[...] == patch_of, 1.0, 0.0)
    picked = dot(jnp.transpose(chosen)[0:VMAX, :].astype(BF16), patches[...])
    raw[...] = picked.astype(BF16)
    slots[0] = layer_norm(picked).astype(BF16)

    for copy in pack_loads:
        copy.wait()
    packed[pl.ds(PRED_AT, 32), :] = jnp.concatenate([pred[...], jnp.zeros((32, LANES - PIX), BF16)], axis=1)
    packed[pl.ds(PRED_AT + 32, HALF - PRED_AT - 32), :] = jnp.zeros((HALF - PRED_AT - 32, LANES), BF16)
    pl.semaphore_wait(barrier, len(greeted))

    def send(src, dst, sems, index, device):
        copy = pltpu.make_async_remote_copy(
            src_ref=src, dst_ref=dst, send_sem=sems[0].at[index], recv_sem=sems[1].at[index],
            device_id=device, device_id_type=MESH,
        )
        copy.start()
        return copy

    sent = []

    def send_all(items, sems, first):
        copies = [send(src, dst, sems, first + i, device) for i, (src, dst, device) in enumerate(items)]
        sent.extend(copies)
        return copies

    def arrive(copies):
        for copy in copies:
            copy.wait_recv()

    wsem, dsem, rsem, bsem = (w_send, w_recv), (d_send, d_recv), (r_send, r_recv), (b_send, b_recv)

    def up_at(piece, count):
        return pl.ds(pl.multiple_of(piece * UP_PIECE, 16), count * UP_PIECE)

    def group(i, count):
        return pl.ds(pl.multiple_of(i * 48, 16), count * 48)

    cell = (group(c * 4 + x, 1), pl.ds(pl.multiple_of(y * SHARD, LANES), SHARD))
    w0 = send_all(
        [(w_up.at[up_at(q_x, 1)], up2.at[up_at(q_x, 1)], at_z(8)), (w_down.at[cell], down2.at[cell], at_z(8))],
        wsem, 0,
    )

    mine = z_slot(z)
    same_class = pl.ds(pl.multiple_of(cls * 4, 4), 4)
    low, high = pl.ds(0, 8), pl.ds(8, 8)
    gathers = {}

    def gather(half, step):
        def at(piece, count):
            return pl.ds(pl.multiple_of(half * HALF + piece * 16, 16), count * 16)

        def same(slots_z, rows_p, device):
            return (dec.at[slots_z, rows_p], dec.at[slots_z, rows_p], device)

        if step:
            arrive(gathers[half, step - 1])
        if step == 0:
            dec[mine, at(q_z, 1), :] = packed[at(q_z, 1), :]
            items = [(packed.at[at(q_z, 1)], dec.at[mine, at(q_z, 1)], at_z(s)) for s in (4, 8, 12)]
        elif step == 1:
            items = [same(same_class, at(q_z, 1), at_z(s)) for s in (1, 2, 3)]
        elif step == 2:
            items = [same(low, at(q_x, 1), at_x(s)) for s in (1, 2, 3)]
            items += [same(high, at(q_y, 1), at_y(s)) for s in (1, 2, 3)]
        elif step == 3:
            items = [same(low, at(q_xs, 4), at_y(s)) for s in (1, 2, 3)]
            items += [same(high, at(q_ys, 4), at_x(s)) for s in (1, 2, 3)]
        elif step == 4:
            items = [(dec.at[:, at(c * 16, 16)], dec.at[:, at(c * 16, 16)], other_core)]
        else:
            return
        gathers[half, step] = send_all(items, dsem, half * 19 + (0, 3, 6, 12, 18)[step])

    gather(0, 0)

    def slot_of(k, side):
        return 0 if k == 0 else (7 if k == 4 else 2 * k - 1 + side)

    def send_rows(k, side):
        src, dst = slot_of(k - 1, side), slot_of(k, side)
        return [
            (slots.at[src, pl.ds(at, n)], slots.at[dst, pl.ds(at, n)], ahead if side == 0 else behind)
            for at, n in CHUNKS
        ]

    def row_sem(k, side):
        return 2 * (slot_of(k, side) - 1)

    rows = {}

    def start_rows(k, side):
        rows[k, side] = send_all(send_rows(k, side), rsem, row_sem(k, side))

    def pass_rows(k):
        todo = [side for side in (0, 1) if (k, side) in rows]
        items = {side: send_rows(k + 1, side) for side in todo if k + 1 <= (3, 4)[side]}
        for side in items:
            rows[k + 1, side] = []
        for i in range(len(CHUNKS)):
            for side in todo:
                rows[k, side][i].wait_recv()
                if side in items:
                    rows[k + 1, side] += send_all([items[side][i]], rsem, row_sem(k + 1, side) + i)

    def weight(at, rows_per, blocks):
        return jnp.concatenate(
            [
                jnp.concatenate(
                    [dec[z_slot(s), at + b * rows_per : at + (b + 1) * rows_per, :] for s in range(NZ)], axis=0
                )
                for b in blocks
            ],
            axis=1,
        )

    def hide(slot, count=1):
        block = slots[slot : slot + count].reshape(count * VMAX, D)
        part = gelu(dot(block, up[...])).astype(BF16)
        hidden[slot : slot + count, :, 0:SHARD] = part.reshape(count, VMAX, SHARD)

    def hide_far(i, carry):
        block = slots[pl.ds(2 * i, 2)].reshape(2 * VMAX, D)
        part = gelu(dot(block, up2[...])).astype(BF16)
        hidden[pl.ds(2 * i, 2), :, SHARD : 2 * SHARD] = part.reshape(2, VMAX, SHARD)
        return carry

    start_rows(1, 0)
    start_rows(1, 1)
    up_load.wait()
    hide(0)
    gather(0, 1)
    pass_rows(1)
    arrive(w0)
    w1 = send_all(
        [(up2.at[up_at(q_x, 1)], up2.at[up_at(q_x, 1)], at_x(s)) for s in (1, 2, 3)]
        + [(down2.at[cell], down2.at[cell], at_y(s)) for s in (1, 2, 3)],
        wsem, 2,
    )
    gather(0, 2)
    pass_rows(2)
    arrive(w1)
    w2 = send_all(
        [(up2.at[up_at(q_xs, 4)], up2.at[up_at(q_xs, 4)], at_y(s)) for s in (1, 2, 3)]
        + [(down2.at[group(c * 4 + x, 1)], down2.at[group(c * 4 + x, 1)], at_x(s)) for s in (1, 2, 3)],
        wsem, 8,
    )
    gather(0, 3)
    hide(1, 2)
    pass_rows(3)
    hide(3, 2)
    gather(1, 0)
    hide(5, 2)
    gather(1, 1)
    down_load.wait()
    for copy in late_loads:
        copy.wait()
    arrive(w2)
    w3 = send_all(
        [
            (up2.at[up_at(c * 16, 16)], up2.at[up_at(c * 16, 16)], other_core),
            (down2.at[group(c * 4, 4)], down2.at[group(c * 4, 4)], other_core),
        ],
        wsem, 14,
    )
    gather(0, 4)
    gather(1, 2)
    arrive(w3)
    lax.fori_loop(0, 3, hide_far, 0)
    gather(0, 5)
    for half in (0, 1):
        embed = weight(EMBED_AT, 96, (2 * half, 2 * half + 1))
        cols = slice(256 * half, 256 * half + 256)
        for s, shard in enumerate((down, down2)):
            w2e[s * SHARD : (s + 1) * SHARD, cols] = dot(shard[...], embed).astype(BF16)
        own[:, cols] = dot(raw[...], embed)
    pass_rows(4)
    hide(7)
    hide_far(3, 0)
    gather(1, 3)

    def partial(slot):
        return dot(hidden[slot], w2e[...])

    back = {}
    wide = DD // 2

    def hand_back(side, step, value):
        i = side * 3 + step
        to = behind if side == 0 else ahead
        back[side, step] = []
        for h in (0, 1):
            if step:
                arrive([back[side, step - 1][h]])
                ret_out[i, h] = (ret_in[i - 1, h].astype(F32) + part[value, :, h * wide : (h + 1) * wide]).astype(BF16)
            else:
                ret_out[i, h] = value[:, h * wide : (h + 1) * wide].astype(BF16)
            back[side, step] += send_all([(ret_out.at[i, h], ret_in.at[i, h], to)], bsem, 2 * i + h)

    hand_back(1, 0, partial(slot_of(4, 1)))
    hand_back(0, 0, partial(slot_of(3, 0)))
    own[...] += partial(0)

    def add_part(slot, carry):
        part[slot] = partial(slot)
        return carry

    lax.fori_loop(1, 7, add_part, 0)
    for step in (1, 2, 3):
        hand_back(1, step, slot_of(4 - step, 1))
        if step < 3:
            hand_back(0, step, slot_of(3 - step, 0))
    gather(1, 4)

    count = visible[0]
    row = lax.broadcasted_iota(jnp.int32, (N_PATCH, N_PATCH), 0)
    lane = lax.broadcasted_iota(jnp.int32, (N_PATCH, N_PATCH), 1)
    patch = 4 * (row % 32) + row // 32
    spread = jnp.where((keep[...] == patch) & (lane < count), 1.0, 0.0)
    seen = jnp.sum(spread, axis=1, keepdims=True) > 0.5
    spread = spread[:, 0:VMAX].astype(BF16)
    order = jnp.where(lane == patch, 1.0, 0.0)
    places = dot(order.astype(BF16), position[...])
    masked = mask_token[...].astype(F32).reshape(1, DD)

    arrive(back[0, 2])
    arrive(back[1, 3])
    returned = [ret_in[2, h].astype(F32) + ret_in[6, h].astype(F32) for h in (0, 1)]
    embedded = (own[...] + jnp.concatenate(returned, axis=1)).astype(BF16)
    gather(1, 5)
    start = jnp.where(seen, dot(spread, embedded), masked) + places
    normed = layer_norm(start).astype(BF16)
    for b in range(6):
        both = dot(normed, weight(QKV_AT, 32, (2 * b, 2 * b + 1))).astype(BF16)
        proj[2 * b] = both[:, 0:LANES]
        proj[2 * b + 1] = both[:, LANES : 2 * LANES]
    left = lane < HSIZE
    for b in range(4):
        query, keys, values = proj[b], proj[4 + b], proj[8 + b]
        outs = []
        for side in (left, jnp.logical_not(left)):
            one = jnp.where(side, query.astype(F32), 0.0).astype(BF16)
            scores = lax.dot_general(one, keys, (((1,), (1,)), ((), ())), preferred_element_type=F32)
            scores = scores * (1.0 / math.sqrt(HSIZE))
            weights = jnp.exp(scores - jnp.max(scores, axis=-1, keepdims=True))
            probs = (weights / jnp.sum(weights, axis=-1, keepdims=True)).astype(BF16)
            outs.append(dot(probs, values))
        mixed[:, b * LANES : (b + 1) * LANES] = jnp.where(left, outs[0], outs[1]).astype(BF16)
    after = start + jnp.concatenate(
        [dot(mixed[...], weight(OUT_AT, 32, (2 * b, 2 * b + 1))) for b in range(2)], axis=1
    )
    final = layer_norm(after).astype(BF16)
    prediction = dot(final, weight(PRED_AT, 32, (0,)))

    turned = [pltpu.roll(prediction[32 * r : 32 * r + 32, :], (PIX * r) % LANES, 1) if r else prediction[0:32, :] for r in range(4)]
    lane = lane[0:32, :]
    edges = (96, 64, 32)
    pixels = [jnp.where(lane < edges[b], turned[b], turned[b + 1]) for b in range(3)]
    sums = [0.0] * 4
    for b in range(3):
        wide = pixels[b].astype(BF16)
        wanted = []
        for g in range(32):
            at = slice(384 * g + LANES * b, 384 * g + LANES * b + LANES)
            recon[:, at] = wide[g : g + 1, :]
            wanted.append(targets[:, at])
        error = pixels[b] - jnp.concatenate(wanted, axis=0).astype(F32)
        error = error * error
        sums[b] += jnp.sum(jnp.where(lane < edges[b], error, 0.0), axis=-1, keepdims=True)
        sums[b + 1] += jnp.sum(jnp.where(lane < edges[b], 0.0, error), axis=-1, keepdims=True)
    per_row = jnp.where(seen, 0.0, jnp.concatenate(sums, axis=0) * (1.0 / PIX))
    loss[...] = jnp.sum(order * per_row, axis=0, keepdims=True)

    for copy in sent:
        copy.wait_send()


def body(
    patches, keep_index, visible, targets, w_up, w_down, dec_embed, dec_qkv, dec_out, dec_pred, mask_token, position
):
    hbm = pl.BlockSpec(memory_space=pltpu.HBM)
    vmem = pl.BlockSpec(memory_space=pltpu.VMEM)
    dma = pltpu.SemaphoreType.DMA
    return pl.pallas_call(
        kernel,
        out_shape=(
            jax.ShapeDtypeStruct((1, N_PATCH * PIX), BF16),
            jax.ShapeDtypeStruct((1, N_PATCH), F32),
        ),
        in_specs=[hbm] * 12,
        out_specs=(vmem, vmem),
        scratch_shapes=[
            pltpu.SMEM((1,), jnp.int32),
            pltpu.VMEM((1, N_PATCH), jnp.int32),
            pltpu.VMEM((N_PATCH, D), BF16),
            pltpu.VMEM((1, N_PATCH * PIX), BF16),
            pltpu.VMEM((DD,), BF16),
            pltpu.VMEM((N_PATCH, DD), BF16),
            pltpu.VMEM((32, PIX), BF16),
            pltpu.VMEM((D, SHARD), BF16),
            pltpu.VMEM((SHARD, D), BF16),
            pltpu.VMEM((PACKED, LANES), BF16),
            pltpu.VMEM((D, SHARD), BF16),
            pltpu.VMEM((SHARD, D), BF16),
            pltpu.VMEM((NZ, PACKED, LANES), BF16),
            pltpu.VMEM((VMAX, D), BF16),
            pltpu.VMEM((8, VMAX, D), BF16),
            pltpu.VMEM((8, VMAX, 2 * SHARD), BF16),
            pltpu.VMEM((2 * SHARD, DD), BF16),
            pltpu.VMEM((8, VMAX, DD), F32),
            pltpu.VMEM((VMAX, DD), F32),
            pltpu.VMEM((7, 2, VMAX, DD // 2), BF16),
            pltpu.VMEM((7, 2, VMAX, DD // 2), BF16),
            pltpu.VMEM((12, N_PATCH, LANES), BF16),
            pltpu.VMEM((N_PATCH, DD), BF16),
            dma((29,)),
            dma((16,)),
            dma((16,)),
            dma((38,)),
            dma((38,)),
            dma((14,)),
            dma((14,)),
            dma((14,)),
            dma((14,)),
        ],
        compiler_params=pltpu.CompilerParams(
            collective_id=0, has_side_effects=True, vmem_limit_bytes=56 * 1024 * 1024
        ),
    )(
        visible, keep_index, patches, targets, mask_token, position,
        w_up, w_down, dec_embed, dec_qkv, dec_out, dec_pred,
    )


def solution(mesh):
    return jax.shard_map(
        body,
        mesh=mesh,
        in_specs=(
            P(("dp", "mp"), None, None),
            P(("dp", "mp"), None),
            P(("dp", "mp")),
            P(("dp", "mp"), None),
            P(None, "mp"),
            P("mp", None),
            P("mp", None),
            P("mp", None),
            P("mp", None),
            P("mp", None),
            P(),
            P(),
        ),
        out_specs=(P(("dp", "mp"), None), P(("dp", "mp"), None)),
        check_vma=False,
    )
```

```python
import functools
import math

import jax
import jax.numpy as jnp
from jax import lax
from jax.experimental import pallas as pl
from jax.experimental.pallas import tpu as pltpu
from jax.sharding import PartitionSpec as P

D = 1536
DD = 512
HSIZE = 64
PIX = 96
VMAX = 80
N_PATCH = 128
NZ = 16
SHARD = 384
LANES = 128
EPSILON = 1e-06
MESH = pl.DeviceIdType.MESH
F32 = jnp.float32
BF16 = jnp.bfloat16

EMBED_AT = 0
PRED_AT = 384
QKV_AT = 512
OUT_AT = 896
PACKED = 1024
HALF = 512

UP_PIECE = 48
CHUNKS = ((0, 48), (48, 32))


def z_slot(z):
    return (z % 4) * 4 + z // 4


def layer_norm(values):
    center = values - jnp.mean(values, axis=-1, keepdims=True)
    spread = jnp.mean(center * center, axis=-1, keepdims=True)
    return center * lax.rsqrt(spread + EPSILON)


def gelu(v):
    return 0.5 * v * (1.0 + jnp.tanh(math.sqrt(2.0 / math.pi) * (v + 0.044715 * v * v * v)))


def dot(a, b):
    return jnp.dot(a, b, preferred_element_type=F32)


def kernel(
    visible_hbm, keep_hbm, patches_hbm, targets_hbm, mask_hbm, position_hbm,
    w_up, w_down, d_embed, d_qkv, d_out, d_pred,
    recon, loss,
    visible, keep, patches, targets, mask_token, position, pred,
    up, down, packed, up2, down2, dec, raw, slots, hidden, w2e, part, own, ret_out, ret_in, proj, mixed,
    load_sem, w_send, w_recv, d_send, d_recv, r_send, r_recv, b_send, b_recv,
):
    dp, z = lax.axis_index("dp"), lax.axis_index("mp")
    x, y, c = dp // 8, (dp // 2) % 4, dp % 2
    sign = 1 - 2 * c
    q_x = c * 16 + y * 4 + x
    q_y = c * 16 + x * 4 + y
    cls = z % 4
    q_z = jnp.where(cls < 2, q_x, q_y)
    q_xs, q_ys = c * 16 + y * 4, c * 16 + x * 4

    def at_z(step):
        return (dp, (z + step + 2 * NZ) % NZ)

    def at_x(step):
        return (((x + step) % 4) * 8 + y * 2 + c, z)

    def at_y(step):
        return (x * 8 + ((y + step) % 4) * 2 + c, z)

    other_core = (x * 8 + y * 2 + (1 - c), z)
    ahead, behind = at_z(sign), at_z(-sign)

    barrier = pltpu.get_barrier_semaphore()
    greeted = [at_z(s) for s in (8, 4, 12, 3, 13, 2, 14, 1, 15)]
    greeted += [at_x(s) for s in (2, 1, 3)] + [at_y(s) for s in (2, 1, 3)] + [other_core]
    for device in greeted:
        pl.semaphore_signal(barrier, inc=1, device_id=device, device_id_type=MESH)

    n_loads = [0]

    def load(src, dst):
        copy = pltpu.make_async_copy(src, dst, load_sem.at[n_loads[0]])
        n_loads[0] += 1
        copy.start()
        return copy

    first_loads = [load(keep_hbm, keep), load(patches_hbm.at[0], patches)]
    pack_loads = [
        load(d_embed.at[:, pl.ds(j * LANES, LANES)], packed.at[pl.ds(EMBED_AT + j * 96, 96)]) for j in range(4)
    ]
    pack_loads += [
        load(d_qkv.at[:, pl.ds(j * LANES, LANES)], packed.at[pl.ds(QKV_AT + j * 32, 32)]) for j in range(12)
    ]
    pack_loads += [
        load(d_out.at[:, pl.ds(j * LANES, LANES)], packed.at[pl.ds(OUT_AT + j * 32, 32)]) for j in range(4)
    ]
    pack_loads += [load(d_pred, pred)]
    up_load, down_load = load(w_up, up), load(w_down, down)
    late_loads = [
        load(visible_hbm, visible), load(targets_hbm, targets), load(mask_hbm, mask_token), load(position_hbm, position)
    ]

    for copy in first_loads:
        copy.wait()
    patch_of = lax.broadcasted_iota(jnp.int32, (N_PATCH, N_PATCH), 0)
    chosen = jnp.where(keep[...] == patch_of, 1.0, 0.0)
    picked = dot(jnp.transpose(chosen)[0:VMAX, :].astype(BF16), patches[...])
    raw[...] = picked.astype(BF16)
    slots[0] = layer_norm(picked).astype(BF16)

    for copy in pack_loads:
        copy.wait()
    packed[pl.ds(PRED_AT, 32), :] = jnp.concatenate([pred[...], jnp.zeros((32, LANES - PIX), BF16)], axis=1)
    packed[pl.ds(PRED_AT + 32, HALF - PRED_AT - 32), :] = jnp.zeros((HALF - PRED_AT - 32, LANES), BF16)
    pl.semaphore_wait(barrier, len(greeted))

    def send(src, dst, sems, index, device):
        copy = pltpu.make_async_remote_copy(
            src_ref=src, dst_ref=dst, send_sem=sems[0].at[index], recv_sem=sems[1].at[index],
            device_id=device, device_id_type=MESH,
        )
        copy.start()
        return copy

    sent = []

    def send_all(items, sems, first):
        copies = [send(src, dst, sems, first + i, device) for i, (src, dst, device) in enumerate(items)]
        sent.extend(copies)
        return copies

    def arrive(copies):
        for copy in copies:
            copy.wait_recv()

    wsem, dsem, rsem, bsem = (w_send, w_recv), (d_send, d_recv), (r_send, r_recv), (b_send, b_recv)

    def up_at(piece, count):
        return pl.ds(pl.multiple_of(piece * UP_PIECE, 16), count * UP_PIECE)

    def group(i, count):
        return pl.ds(pl.multiple_of(i * 48, 16), count * 48)

    cell = (group(c * 4 + x, 1), pl.ds(pl.multiple_of(y * SHARD, LANES), SHARD))
    w0 = send_all(
        [(w_up.at[up_at(q_x, 1)], up2.at[up_at(q_x, 1)], at_z(8)), (w_down.at[cell], down2.at[cell], at_z(8))],
        wsem, 0,
    )

    mine = z_slot(z)
    same_class = pl.ds(pl.multiple_of(cls * 4, 4), 4)
    low, high = pl.ds(0, 8), pl.ds(8, 8)
    gathers = {}

    def gather(half, step):
        def at(piece, count):
            return pl.ds(pl.multiple_of(half * HALF + piece * 16, 16), count * 16)

        def same(slots_z, rows_p, device):
            return (dec.at[slots_z, rows_p], dec.at[slots_z, rows_p], device)

        if step:
            arrive(gathers[half, step - 1])
        if step == 0:
            dec[mine, at(q_z, 1), :] = packed[at(q_z, 1), :]
            items = [(packed.at[at(q_z, 1)], dec.at[mine, at(q_z, 1)], at_z(s)) for s in (4, 8, 12)]
        elif step == 1:
            items = [same(same_class, at(q_z, 1), at_z(s)) for s in (1, 2, 3)]
        elif step == 2:
            items = [same(low, at(q_x, 1), at_x(s)) for s in (1, 2, 3)]
            items += [same(high, at(q_y, 1), at_y(s)) for s in (1, 2, 3)]
        elif step == 3:
            items = [same(low, at(q_xs, 4), at_y(s)) for s in (1, 2, 3)]
            items += [same(high, at(q_ys, 4), at_x(s)) for s in (1, 2, 3)]
        elif step == 4:
            items = [(dec.at[:, at(c * 16, 16)], dec.at[:, at(c * 16, 16)], other_core)]
        else:
            return
        gathers[half, step] = send_all(items, dsem, half * 19 + (0, 3, 6, 12, 18)[step])

    gather(0, 0)

    def slot_of(k, side):
        return 0 if k == 0 else (7 if k == 4 else 2 * k - 1 + side)

    def send_rows(k, side):
        src, dst = slot_of(k - 1, side), slot_of(k, side)
        return [
            (slots.at[src, pl.ds(at, n)], slots.at[dst, pl.ds(at, n)], ahead if side == 0 else behind)
            for at, n in CHUNKS
        ]

    def row_sem(k, side):
        return 2 * (slot_of(k, side) - 1)

    rows = {}

    def start_rows(k, side):
        rows[k, side] = send_all(send_rows(k, side), rsem, row_sem(k, side))

    def pass_rows(k):
        todo = [side for side in (0, 1) if (k, side) in rows]
        items = {side: send_rows(k + 1, side) for side in todo if k + 1 <= (3, 4)[side]}
        for side in items:
            rows[k + 1, side] = []
        for i in range(len(CHUNKS)):
            for side in todo:
                rows[k, side][i].wait_recv()
                if side in items:
                    rows[k + 1, side] += send_all([items[side][i]], rsem, row_sem(k + 1, side) + i)

    def weight(at, rows_per, blocks):
        return jnp.concatenate(
            [
                jnp.concatenate(
                    [dec[z_slot(s), at + b * rows_per : at + (b + 1) * rows_per, :] for s in range(NZ)], axis=0
                )
                for b in blocks
            ],
            axis=1,
        )

    def hide(slot, count=1):
        block = slots[slot : slot + count].reshape(count * VMAX, D)
        part = gelu(dot(block, up[...])).astype(BF16)
        hidden[slot : slot + count, :, 0:SHARD] = part.reshape(count, VMAX, SHARD)

    def hide_far(i, carry):
        block = slots[pl.ds(2 * i, 2)].reshape(2 * VMAX, D)
        part = gelu(dot(block, up2[...])).astype(BF16)
        hidden[pl.ds(2 * i, 2), :, SHARD : 2 * SHARD] = part.reshape(2, VMAX, SHARD)
        return carry

    start_rows(1, 0)
    start_rows(1, 1)
    up_load.wait()
    hide(0)
    gather(0, 1)
    pass_rows(1)
    arrive(w0)
    w1 = send_all(
        [(up2.at[up_at(q_x, 1)], up2.at[up_at(q_x, 1)], at_x(s)) for s in (1, 2, 3)]
        + [(down2.at[cell], down2.at[cell], at_y(s)) for s in (1, 2, 3)],
        wsem, 2,
    )
    gather(0, 2)
    pass_rows(2)
    arrive(w1)
    w2 = send_all(
        [(up2.at[up_at(q_xs, 4)], up2.at[up_at(q_xs, 4)], at_y(s)) for s in (1, 2, 3)]
        + [(down2.at[group(c * 4 + x, 1)], down2.at[group(c * 4 + x, 1)], at_x(s)) for s in (1, 2, 3)],
        wsem, 8,
    )
    gather(0, 3)
    gather(1, 0)
    hide(1, 2)
    pass_rows(3)
    gather(1, 1)
    hide(3, 2)
    hide(5, 2)
    down_load.wait()
    for copy in late_loads:
        copy.wait()
    arrive(w2)
    w3 = send_all(
        [
            (up2.at[up_at(c * 16, 16)], up2.at[up_at(c * 16, 16)], other_core),
            (down2.at[group(c * 4, 4)], down2.at[group(c * 4, 4)], other_core),
        ],
        wsem, 14,
    )
    gather(0, 4)
    gather(1, 2)
    arrive(w3)
    lax.fori_loop(0, 3, hide_far, 0)
    gather(0, 5)
    for half in (0, 1):
        embed = weight(EMBED_AT, 96, (2 * half, 2 * half + 1))
        cols = slice(256 * half, 256 * half + 256)
        for s, shard in enumerate((down, down2)):
            w2e[s * SHARD : (s + 1) * SHARD, cols] = dot(shard[...], embed).astype(BF16)
        own[:, cols] = dot(raw[...], embed)
    pass_rows(4)
    hide(7)
    hide_far(3, 0)
    gather(1, 3)

    def partial(slot):
        return dot(hidden[slot], w2e[...])

    back = {}
    wide = DD // 2

    def hand_back(side, step, value):
        i = side * 3 + step
        to = behind if side == 0 else ahead
        back[side, step] = []
        for h in (0, 1):
            if step:
                arrive([back[side, step - 1][h]])
                ret_out[i, h] = (ret_in[i - 1, h].astype(F32) + part[value, :, h * wide : (h + 1) * wide]).astype(BF16)
            else:
                ret_out[i, h] = value[:, h * wide : (h + 1) * wide].astype(BF16)
            back[side, step] += send_all([(ret_out.at[i, h], ret_in.at[i, h], to)], bsem, 2 * i + h)

    hand_back(1, 0, partial(slot_of(4, 1)))
    hand_back(0, 0, partial(slot_of(3, 0)))
    own[...] += partial(0)

    def add_part(slot, carry):
        part[slot] = partial(slot)
        return carry

    lax.fori_loop(1, 7, add_part, 0)
    for step in (1, 2, 3):
        hand_back(1, step, slot_of(4 - step, 1))
        if step < 3:
            hand_back(0, step, slot_of(3 - step, 0))
    gather(1, 4)

    count = visible[0]
    row = lax.broadcasted_iota(jnp.int32, (N_PATCH, N_PATCH), 0)
    lane = lax.broadcasted_iota(jnp.int32, (N_PATCH, N_PATCH), 1)
    patch = 4 * (row % 32) + row // 32
    spread = jnp.where((keep[...] == patch) & (lane < count), 1.0, 0.0)
    seen = jnp.sum(spread, axis=1, keepdims=True) > 0.5
    spread = spread[:, 0:VMAX].astype(BF16)
    order = jnp.where(lane == patch, 1.0, 0.0)
    places = dot(order.astype(BF16), position[...])
    masked = mask_token[...].astype(F32).reshape(1, DD)

    arrive(back[0, 2])
    arrive(back[1, 3])
    returned = [ret_in[2, h].astype(F32) + ret_in[6, h].astype(F32) for h in (0, 1)]
    embedded = (own[...] + jnp.concatenate(returned, axis=1)).astype(BF16)
    gather(1, 5)
    start = jnp.where(seen, dot(spread, embedded), masked) + places
    normed = layer_norm(start).astype(BF16)
    for b in range(6):
        both = dot(normed, weight(QKV_AT, 32, (2 * b, 2 * b + 1))).astype(BF16)
        proj[2 * b] = both[:, 0:LANES]
        proj[2 * b + 1] = both[:, LANES : 2 * LANES]
    left = lane < HSIZE
    for b in range(4):
        query, keys, values = proj[b], proj[4 + b], proj[8 + b]
        outs = []
        for side in (left, jnp.logical_not(left)):
            one = jnp.where(side, query.astype(F32), 0.0).astype(BF16)
            scores = lax.dot_general(one, keys, (((1,), (1,)), ((), ())), preferred_element_type=F32)
            scores = scores * (1.0 / math.sqrt(HSIZE))
            weights = jnp.exp(scores - jnp.max(scores, axis=-1, keepdims=True))
            probs = (weights / jnp.sum(weights, axis=-1, keepdims=True)).astype(BF16)
            outs.append(dot(probs, values))
        mixed[:, b * LANES : (b + 1) * LANES] = jnp.where(left, outs[0], outs[1]).astype(BF16)
    after = start + jnp.concatenate(
        [dot(mixed[...], weight(OUT_AT, 32, (2 * b, 2 * b + 1))) for b in range(2)], axis=1
    )
    final = layer_norm(after).astype(BF16)
    prediction = dot(final, weight(PRED_AT, 32, (0,)))

    turned = [pltpu.roll(prediction[32 * r : 32 * r + 32, :], (PIX * r) % LANES, 1) if r else prediction[0:32, :] for r in range(4)]
    lane = lane[0:32, :]
    edges = (96, 64, 32)
    pixels = [jnp.where(lane < edges[b], turned[b], turned[b + 1]) for b in range(3)]
    sums = [0.0] * 4
    for b in range(3):
        recon[:, LANES * b : LANES * b + LANES] = pixels[b].astype(BF16)
        wanted = []
        for g in range(32):
            at = slice(384 * g + LANES * b, 384 * g + LANES * b + LANES)
            wanted.append(targets[:, at])
        error = pixels[b] - jnp.concatenate(wanted, axis=0).astype(F32)
        error = error * error
        sums[b] += jnp.sum(jnp.where(lane < edges[b], error, 0.0), axis=-1, keepdims=True)
        sums[b + 1] += jnp.sum(jnp.where(lane < edges[b], 0.0, error), axis=-1, keepdims=True)
    per_row = jnp.where(seen, 0.0, jnp.concatenate(sums, axis=0) * (1.0 / PIX))
    loss[...] = jnp.sum(order * per_row, axis=0, keepdims=True)

    for copy in sent:
        copy.wait_send()


def body(
    patches, keep_index, visible, targets, w_up, w_down, dec_embed, dec_qkv, dec_out, dec_pred, mask_token, position
):
    hbm = pl.BlockSpec(memory_space=pltpu.HBM)
    vmem = pl.BlockSpec(memory_space=pltpu.VMEM)
    dma = pltpu.SemaphoreType.DMA
    recon, loss = pl.pallas_call(
        kernel,
        out_shape=(
            jax.ShapeDtypeStruct((32, 4 * PIX), BF16),
            jax.ShapeDtypeStruct((1, N_PATCH), F32),
        ),
        in_specs=[hbm] * 12,
        out_specs=(vmem, vmem),
        scratch_shapes=[
            pltpu.SMEM((1,), jnp.int32),
            pltpu.VMEM((1, N_PATCH), jnp.int32),
            pltpu.VMEM((N_PATCH, D), BF16),
            pltpu.VMEM((1, N_PATCH * PIX), BF16),
            pltpu.VMEM((DD,), BF16),
            pltpu.VMEM((N_PATCH, DD), BF16),
            pltpu.VMEM((32, PIX), BF16),
            pltpu.VMEM((D, SHARD), BF16),
            pltpu.VMEM((SHARD, D), BF16),
            pltpu.VMEM((PACKED, LANES), BF16),
            pltpu.VMEM((D, SHARD), BF16),
            pltpu.VMEM((SHARD, D), BF16),
            pltpu.VMEM((NZ, PACKED, LANES), BF16),
            pltpu.VMEM((VMAX, D), BF16),
            pltpu.VMEM((8, VMAX, D), BF16),
            pltpu.VMEM((8, VMAX, 2 * SHARD), BF16),
            pltpu.VMEM((2 * SHARD, DD), BF16),
            pltpu.VMEM((8, VMAX, DD), F32),
            pltpu.VMEM((VMAX, DD), F32),
            pltpu.VMEM((7, 2, VMAX, DD // 2), BF16),
            pltpu.VMEM((7, 2, VMAX, DD // 2), BF16),
            pltpu.VMEM((12, N_PATCH, LANES), BF16),
            pltpu.VMEM((N_PATCH, DD), BF16),
            dma((29,)),
            dma((16,)),
            dma((16,)),
            dma((38,)),
            dma((38,)),
            dma((14,)),
            dma((14,)),
            dma((14,)),
            dma((14,)),
        ],
        compiler_params=pltpu.CompilerParams(
            collective_id=0, has_side_effects=True, vmem_limit_bytes=56 * 1024 * 1024
        ),
    )(
        visible, keep_index, patches, targets, mask_token, position,
        w_up, w_down, dec_embed, dec_qkv, dec_out, dec_pred,
    )
    return (recon.reshape(1, N_PATCH * PIX), loss)


def solution(mesh):
    return jax.shard_map(
        body,
        mesh=mesh,
        in_specs=(
            P(("dp", "mp"), None, None),
            P(("dp", "mp"), None),
            P(("dp", "mp")),
            P(("dp", "mp"), None),
            P(None, "mp"),
            P("mp", None),
            P("mp", None),
            P("mp", None),
            P("mp", None),
            P("mp", None),
            P(),
            P(),
        ),
        out_specs=(P(("dp", "mp"), None), P(("dp", "mp"), None)),
        check_vma=False,
    )
```
